256 devices in a mesh: lat: 8 (over x, core), lon: 32 (over z, y).
Axes of the slice: x: 4, y: 4, z: 8, core: 2. Of those that a mesh axis runs over, the one named last changes fastest.
Arguments:
- features: float32 [32, 256, 4096], P('lat', None, 'lon'), may hold values from -6 to 6
- basis_panels: float32 [32, 3, 9, 255], P('lat'), may hold values from -0.9 to 0.9
- weights: float32 [9, 256, 256], replicated, may hold values from -0.125 to 0.125
- bias_term: float32 [256], replicated, may hold values from -3 to 3
- widths: int32 [32], P('lat'), may hold values from 4 to 127, as said below
- tap_rows: int32 [32, 3], P('lat'), may hold values from -4 to 4, as said below
Outputs:
- convolved: float32 [32, 256, 4096], P('lat', None, 'lon')
The draws below stay inside these ranges and needn't reach their ends.
Inputs may be any that keep to these rules, and one draw needn't show every extreme that they name: With d = min(i, 31 - i) the distance of row i from the nearer pole, widths[i] is at most min(8 * 32 // (4 * d + 2) + 4, 127), and the first and the last row have the half-width 127. In each aligned block of 4 rows the row nearest a pole has exactly this bound. `tap_rows`: the first row's first tap has the offset -4 and the last row's last tap the offset 4.
All inputs are finite; a program needn't handle non-finite values.
Results may differ from the reference program's by a relative error of at most 0.000062.
Values sent between devices are 32-bit elements; how exact they have to be, the bound alone decides.
A program may use at most 256 MiB of HBM per device.

```python
import jax
import jax.numpy as jnp
from jax import lax

C = 256
K = 9
TAPS = 3
REACH = 4
ROWS = 4
NLAT = 32
NLON = 4096
WMAX = 127
SPAN = 255


def draw_widths(key, part):
    row_ids = jnp.arange(NLAT, dtype=jnp.int32)
    distance = jnp.minimum(row_ids, NLAT - 1 - row_ids)
    base_width = 8 * NLAT // (4 * distance + 2)
    block_nearest = jnp.repeat(jnp.min(distance.reshape(NLAT // ROWS, ROWS), axis=1), ROWS)
    jitter = jax.random.randint(key, (NLAT,), 0, 5, dtype=jnp.int32)
    jitter = jnp.where(distance == block_nearest, 4, jitter)
    result = jnp.minimum(base_width + jitter, WMAX)
    result = jnp.where(distance == 0, WMAX, result)
    return result.astype(jnp.int32)


def draw_tap_rows(key, part):
    offsets = jax.random.randint(key, (NLAT, TAPS), -REACH, REACH + 1, dtype=jnp.int32)
    offsets = offsets.at[0, 0].set(-REACH)
    offsets = offsets.at[NLAT - 1, TAPS - 1].set(REACH)
    return offsets.astype(jnp.int32)


def block_scale(stream_key, extent, cuts, smallest, high):
    gain, own = 1.0, jax.random.fold_in(stream_key, 6)
    for axis_at, blocks in cuts:
        heights = jnp.exp(jax.random.uniform(jax.random.fold_in(own, axis_at), (blocks,), jnp.float32, smallest / len(cuts), high / len(cuts)))
        gain = gain * jnp.repeat(heights, extent[axis_at] // blocks).reshape([-1 if axis == axis_at else 1 for axis in range(len(extent))])
    return gain


def centred(own_key, dims, width, reach, split=(), held_as=jnp.bfloat16):
    factor_of = block_scale(own_key, dims, split, -0.22, 0.18) if split else 1.0
    array = jax.random.normal(own_key, dims, jnp.float32) * width * factor_of
    return jnp.minimum(jnp.maximum(array, -reach), reach).astype(held_as)


def setup_inputs(seed: int = 0) -> dict:
    arg_keys = jax.random.split(jax.random.key(seed), 7)
    return {
        "features": centred(arg_keys[0], (NLAT, C, NLON), 1.0, 6.0, ((0, 8), (2, 32)), jnp.float32),
        "basis_panels": centred(arg_keys[1], (NLAT, TAPS, K, SPAN), 0.15, 0.9, ((0, 8),), jnp.float32),
        "weights": centred(arg_keys[2], (K, C, C), (C * K) ** -0.5, 0.125, (), jnp.float32),
        "bias_term": centred(arg_keys[3], (C,), 0.5, 3.0, (), jnp.float32),
        "widths": draw_widths(jax.random.fold_in(arg_keys[6], 71), 0),
        "tap_rows": draw_tap_rows(jax.random.fold_in(arg_keys[6], 71), 0),
    }


def reference(features, basis_panels, weights, bias_term, widths, tap_rows):
    half_turn = NLON // 2
    top_rows = jnp.roll(features[:REACH][::-1], -half_turn, axis=2)
    low_rows = jnp.roll(features[-REACH:][::-1], -half_turn, axis=2)
    extended = jnp.concatenate([top_rows, features, low_rows], axis=0)
    offsets = jnp.arange(SPAN, dtype=jnp.int32) - WMAX
    inside_band = jnp.abs(offsets)[None, :] <= widths[:, None]
    masked = jnp.where(inside_band[:, None, None, :], basis_panels, jnp.zeros((), basis_panels.dtype))
    places = jnp.mod(offsets, NLON).astype(jnp.int32)
    kernels = jnp.zeros((NLAT, TAPS, K, NLON), basis_panels.dtype).at[:, :, :, places].set(masked)

    def one_row(row_index):
        chosen = jnp.take(extended, row_index + REACH + tap_rows[row_index], axis=0)
        spectrum = jnp.fft.rfft(chosen, axis=-1)
        response = jnp.fft.rfft(kernels[row_index], axis=-1)
        product = jnp.einsum("tkf,tcf->ckf", jnp.conj(response), spectrum)
        spatial = jnp.fft.irfft(product, n=NLON, axis=-1)
        mixed = jnp.einsum("koc,ckl->ol", weights, spatial, precision=lax.Precision.HIGHEST)
        return mixed + bias_term[:, None]

    return lax.map(one_row, jnp.arange(NLAT, dtype=jnp.int32))
```

```python
import functools

import jax
import jax.numpy as jnp
from jax import lax
from jax.experimental import pallas as pl
from jax.experimental.pallas import tpu as pltpu
from jax.sharding import PartitionSpec as P

ROWS = 4
TAPS = 3
K = 9
SPAN = 255
WMAX = 127
L = 128
HALO = (128, 48, 32, 32)
BASE = (0, 128, 176, 208)
HALOS = 240
MESH = pl.DeviceIdType.MESH
NT = (((1,), (1,)), ((), ()))


def split(x):
    high = x.astype(jnp.bfloat16)
    low = (x - high.astype(jnp.float32)).astype(jnp.bfloat16)
    return high, low


def kernel(
    lats, lons,
    widths, taps, bias, basis, feat, weights,
    out,
    ext, wf, wh, wl, panel, bands, t0, t1, t2, t3, xs, ch, cl, acc, hsend, hrecv,
    send_sem, recv_sem, hsend_sem, hrecv_sem, own_sem, w_sem,
):
    la, lo = lax.axis_index("lat"), lax.axis_index("lon")
    channels = ext.shape[1]
    east = {"lat": la, "lon": lax.rem(lo + 1, lons)}
    west = {"lat": la, "lon": lax.rem(lo + lons - 1, lons)}
    half = {"lat": la, "lon": lax.rem(lo + lons // 2, lons)}
    above = {"lat": lax.rem(la + lats - 1, lats), "lon": lo}
    below = {"lat": lax.rem(la + 1, lats), "lon": lo}
    first, last = la == 0, la == lats - 1

    barrier = pltpu.get_barrier_semaphore()

    def greet(peer):
        pl.semaphore_signal(barrier, inc=1, device_id=peer, device_id_type=MESH)

    greet(east)
    greet(west)

    @pl.when(first)
    def _():
        greet(half)

    @pl.when(jnp.logical_not(first))
    def _():
        greet(above)

    @pl.when(last)
    def _():
        greet(half)

    @pl.when(jnp.logical_not(last))
    def _():
        greet(below)

    own = pltpu.make_async_copy(feat, ext.at[pl.ds(ROWS, ROWS)], own_sem)
    fetch = pltpu.make_async_copy(weights, wf, w_sem)
    own.start()
    fetch.start()
    pl.semaphore_wait(barrier, 4)

    def send(src, dst, place, peer):
        return pltpu.make_async_remote_copy(
            src_ref=feat.at[src], dst_ref=ext.at[dst], send_sem=send_sem.at[place],
            recv_sem=recv_sem.at[dst], device_id=peer, device_id_type=MESH,
        )

    @pl.when(first)
    def _():
        for r in range(ROWS):
            send(r, ROWS - 1 - r, r, half).start()

    @pl.when(last)
    def _():
        for r in range(ROWS):
            send(r, 3 * ROWS - 1 - r, ROWS + r, half).start()

    @pl.when(jnp.logical_not(first))
    def _():
        for r in range(ROWS):
            send(r, 2 * ROWS + r, r, above).start()

    @pl.when(jnp.logical_not(last))
    def _():
        for r in range(ROWS):
            send(r, r, ROWS + r, below).start()

    flip = la // (lats // 2)
    rows = [s + flip * (ROWS - 1 - 2 * s) for s in range(ROWS)]
    tables = (t0, t1, t2, t3)

    panel[...] = jnp.zeros_like(panel)
    offset = jnp.abs(lax.broadcasted_iota(jnp.int32, (K, SPAN), 1) - WMAX)
    for s in range(ROWS):
        inside = offset <= widths[rows[s]]
        for t in range(TAPS):
            panel[:, pl.ds(0, SPAN)] = jnp.where(inside, basis[rows[s], t], 0.0)
            bands[TAPS * s + t] = pltpu.roll(panel[...], 2 * L - WMAX, 1)

    line = lax.broadcasted_iota(jnp.int32, (L, L), 0)
    lane = lax.broadcasted_iota(jnp.int32, (L, L), 1)

    for s in range(ROWS):
        h, table = HALO[s], tables[s]

        def fill(k, carry, s=s, h=h, table=table):
            for t in range(TAPS):
                band = jnp.broadcast_to(bands[TAPS * s + t, pl.ds(k, 1), :], (L, 2 * L))
                band = pltpu.roll(band, 0, 1, stride=1, stride_axis=0)
                centre, side = band[:, :L], band[:, L:]
                if h == L:
                    to_west = jnp.where(lane < line, side, 0.0)
                    to_east = jnp.where(lane > line, side, 0.0)
                else:
                    to_west, to_east = side[L - h :], side[:h]
                for at, part in ((0, to_west), (h, to_east), (2 * h, centre)):
                    high, low = split(part)
                    size = part.shape[0]
                    table[k, pl.ds(at, size), pl.ds(L * t, L)] = high
                    table[k, pl.ds(at, size), pl.ds(L * (TAPS + t), L)] = low
            return carry

        lax.fori_loop(0, K, fill, 0)

    fetch.wait()

    def weigh(k, carry):
        high, low = split(wf[k])
        wh[:, pl.ds(pl.multiple_of(k * channels, channels), channels)] = high
        wl[:, pl.ds(pl.multiple_of(k * channels, channels), channels)] = low
        return carry

    lax.fori_loop(0, K, weigh, 0)

    own.wait()
    for r in range(ROWS):
        for dst in (r, 2 * ROWS + r):
            send(r, dst, r, east).wait_recv()

    for s in range(ROWS):
        for t in range(TAPS):
            high, low = split(ext[rows[s] + ROWS + taps[rows[s], t]])
            xs[s, :, pl.ds(L * t, L)] = high
            xs[s, :, pl.ds(L * (TAPS + t), L)] = high
            xs[s, :, pl.ds(L * (2 * TAPS + t), L)] = low

    def convolve(s, start, size):
        def correlate(k, carry):
            band = tables[s][k, pl.ds(start, size), :]
            band = jnp.concatenate([band, band[:, : TAPS * L]], axis=1)
            value = lax.dot_general(band, xs[s], NT, preferred_element_type=jnp.float32)
            high, low = split(value)
            place = pl.ds(pl.multiple_of(k * channels, channels), channels)
            ch[pl.ds(0, size), place] = high
            cl[pl.ds(0, size), place] = low
            return carry

        lax.fori_loop(0, K, correlate, 0)
        high, low = ch[pl.ds(0, size), :], cl[pl.ds(0, size), :]
        dot = functools.partial(lax.dot_general, dimension_numbers=NT, preferred_element_type=jnp.float32)
        return dot(high, wh[...]) + dot(high, wl[...]) + dot(low, wh[...])

    def halo(side, s):
        span = pl.ds(BASE[s], HALO[s])
        return pltpu.make_async_remote_copy(
            src_ref=hsend.at[side, span], dst_ref=hrecv.at[side, span], send_sem=hsend_sem.at[side, s],
            recv_sem=hrecv_sem.at[side, s], device_id=(west, east)[side], device_id_type=MESH,
        )

    def hand_over(s, value):
        h = HALO[s]
        for side in range(2):
            hsend[side, pl.ds(BASE[s], h), :] = value[side * h : side * h + h]
            halo(side, s).start()

    hand_over(0, convolve(0, 0, 2 * L))
    for s in range(1, ROWS):
        h = HALO[s]
        value = convolve(s, 0, 2 * h + L)
        hand_over(s, value)
        acc[s] = value[2 * h :]
    acc[0] = convolve(0, 2 * L, L)

    for s in range(ROWS):
        h = HALO[s]
        for side in range(2):
            halo(side, s).wait_recv()
        acc[s, pl.ds(L - h, h), :] += hrecv[0, pl.ds(BASE[s], h), :]
        acc[s, pl.ds(0, h), :] += hrecv[1, pl.ds(BASE[s], h), :]
        out[rows[s]] = jnp.transpose(acc[s] + bias[...])

    for r in range(ROWS):
        send(r, r, r, east).wait_send()
        send(r, r, ROWS + r, east).wait_send()
    for s in range(ROWS):
        for side in range(2):
            halo(side, s).wait_send()


def per_device(lats, lons, features, basis_panels, weights, bias_term, widths, tap_rows):
    channels = features.shape[1]
    bf16, f32 = jnp.bfloat16, jnp.float32
    vmem, smem = pl.BlockSpec(memory_space=pltpu.VMEM), pl.BlockSpec(memory_space=pltpu.SMEM)
    anywhere = pl.BlockSpec(memory_space=pl.ANY)
    return pl.pallas_call(
        functools.partial(kernel, lats, lons),
        out_shape=jax.ShapeDtypeStruct(features.shape, f32),
        in_specs=[smem, smem, vmem, vmem, anywhere, anywhere],
        out_specs=vmem,
        scratch_shapes=[
            pltpu.VMEM((3 * ROWS, channels, L), f32),
            pltpu.VMEM(weights.shape, f32),
            pltpu.VMEM((channels, K * channels), bf16),
            pltpu.VMEM((channels, K * channels), bf16),
            pltpu.VMEM((K, 2 * L), f32),
            pltpu.VMEM((ROWS * TAPS, K, 2 * L), f32),
            *(pltpu.VMEM((K, 2 * h + L, 2 * TAPS * L), bf16) for h in HALO),
            pltpu.VMEM((ROWS, channels, 3 * TAPS * L), bf16),
            pltpu.VMEM((2 * L, K * channels), bf16),
            pltpu.VMEM((2 * L, K * channels), bf16),
            pltpu.VMEM((ROWS, L, channels), f32),
            pltpu.VMEM((2, HALOS, channels), f32),
            pltpu.VMEM((2, HALOS, channels), f32),
            pltpu.SemaphoreType.DMA((2 * ROWS,)),
            pltpu.SemaphoreType.DMA((3 * ROWS,)),
            pltpu.SemaphoreType.DMA((2, ROWS)),
            pltpu.SemaphoreType.DMA((2, ROWS)),
            pltpu.SemaphoreType.DMA,
            pltpu.SemaphoreType.DMA,
        ],
        compiler_params=pltpu.CompilerParams(
            collective_id=0, has_side_effects=True, vmem_limit_bytes=56 << 20
        ),
    )(widths, tap_rows, bias_term[None, :], basis_panels, features, weights)


def solution(mesh):
    return jax.shard_map(
        functools.partial(per_device, mesh.shape["lat"], mesh.shape["lon"]),
        mesh=mesh,
        in_specs=(
            P("lat", None, "lon"),
            P("lat", None, None, None),
            P(),
            P(),
            P("lat"),
            P("lat", None),
        ),
        out_specs=P("lat", None, "lon"),
        check_vma=False,
    )
```

```python
import functools

import jax
import jax.numpy as jnp
from jax import lax
from jax.experimental import pallas as pl
from jax.experimental.pallas import tpu as pltpu
from jax.sharding import PartitionSpec as P

ROWS = 4
TAPS = 3
K = 9
SPAN = 255
WMAX = 127
L = 128
HALO = (128, 48, 48, 32)
GROUP = (0, 1, 1, 1)
BASE = (0, 0, 48, 96)
MESH = pl.DeviceIdType.MESH
NT = (((1,), (1,)), ((), ()))


def split(x):
    high = x.astype(jnp.bfloat16)
    low = (x - high.astype(jnp.float32)).astype(jnp.bfloat16)
    return high, low


def product(a, b):
    return lax.dot_general(a, b, NT, preferred_element_type=jnp.float32)


def kernel(
    lats, lons,
    widths_in, taps_in, bias_in, basis_in, feat, weights,
    out,
    widths, taps, bias, basis, ext, wf, wh, wl, panel, bands, h0, h1, h2, h3, centre, xs, sides, middle, shift, hsend, hrecv,
    send_sem, recv_sem, hsend_sem, hrecv_sem, own_sem, w_sem, small_sem,
):
    la, lo = lax.axis_index("lat"), lax.axis_index("lon")
    channels = ext.shape[1]
    east = {"lat": la, "lon": lax.rem(lo + 1, lons)}
    west = {"lat": la, "lon": lax.rem(lo + lons - 1, lons)}
    half = {"lat": la, "lon": lax.rem(lo + lons // 2, lons)}
    above = {"lat": lax.rem(la + lats - 1, lats), "lon": lo}
    below = {"lat": lax.rem(la + 1, lats), "lon": lo}
    first, last = la == 0, la == lats - 1

    barrier = pltpu.get_barrier_semaphore()

    def greet(peer):
        pl.semaphore_signal(barrier, inc=1, device_id=peer, device_id_type=MESH)

    greet(east)
    greet(west)

    @pl.when(first)
    def _():
        greet(half)

    @pl.when(jnp.logical_not(first))
    def _():
        greet(above)

    @pl.when(last)
    def _():
        greet(half)

    @pl.when(jnp.logical_not(last))
    def _():
        greet(below)

    small = [
        pltpu.make_async_copy(src, dst, small_sem.at[i])
        for i, (src, dst) in enumerate(((widths_in, widths), (taps_in, taps), (bias_in, bias), (basis_in, basis)))
    ]
    own = pltpu.make_async_copy(feat, ext.at[pl.ds(ROWS, ROWS)], own_sem)
    fetch = pltpu.make_async_copy(weights, wf, w_sem)
    for copy in (*small, own, fetch):
        copy.start()
    pl.semaphore_wait(barrier, 4)

    def send(src, dst, place, peer):
        return pltpu.make_async_remote_copy(
            src_ref=feat.at[src], dst_ref=ext.at[dst], send_sem=send_sem.at[place],
            recv_sem=recv_sem.at[dst], device_id=peer, device_id_type=MESH,
        )

    @pl.when(first)
    def _():
        for r in range(ROWS):
            send(r, ROWS - 1 - r, r, half).start()

    @pl.when(last)
    def _():
        for r in range(ROWS):
            send(r, 3 * ROWS - 1 - r, ROWS + r, half).start()

    @pl.when(jnp.logical_not(first))
    def _():
        for r in range(ROWS):
            send(r, 2 * ROWS + r, r, above).start()

    @pl.when(jnp.logical_not(last))
    def _():
        for r in range(ROWS):
            send(r, r, ROWS + r, below).start()

    flip = la // (lats // 2)
    rows = [s + flip * (ROWS - 1 - 2 * s) for s in range(ROWS)]

    for copy in small:
        copy.wait()
    row = lax.broadcasted_iota(jnp.int32, (ROWS, SPAN), 0)
    limit = jnp.full((ROWS, SPAN), widths[0])
    for r in range(1, ROWS):
        limit = jnp.where(row == r, widths[r], limit)
    inside = jnp.abs(lax.broadcasted_iota(jnp.int32, (ROWS, SPAN), 1) - WMAX) <= limit
    panel[...] = jnp.zeros_like(panel)
    for t in range(TAPS):
        for k in range(K):
            panel[K * t + k, :, pl.ds(0, SPAN)] = jnp.where(inside, basis[t, k], 0.0)
            bands[K * t + k] = pltpu.roll(panel[K * t + k], 2 * L - WMAX, 1)

    line = lax.broadcasted_iota(jnp.int32, (L, L), 0)
    lane = lax.broadcasted_iota(jnp.int32, (L, L), 1)
    beside = (h0, h1, h2, h3)

    for s in range(ROWS):

        def fill(k, carry, s=s, h=HALO[s], table=beside[s]):
            for t in range(TAPS):
                band = jnp.broadcast_to(bands[K * t + k, pl.ds(rows[s], 1), :], (L, 2 * L))
                band = pltpu.roll(band, 0, 1, stride=1, stride_axis=0)
                inner, side = band[:, :L], band[:, L:]
                if h == L:
                    to_west = jnp.where(lane < line, side, 0.0)
                    to_east = jnp.where(lane > line, side, 0.0)
                else:
                    to_west, to_east = side[L - h :], side[:h]
                both = jnp.concatenate([to_west, to_east], axis=0)
                spot = pl.ds(pl.multiple_of(k * 2 * h, 2 * h), 2 * h)
                for part, value in enumerate(split(both)):
                    table[spot, pl.ds(L * (TAPS * part + t), L)] = value
                spot = pl.ds(pl.multiple_of(k * L, L), L)
                for part, value in enumerate(split(inner)):
                    centre[s, spot, pl.ds(L * (TAPS * part + t), L)] = value
            return carry

        lax.fori_loop(0, K, fill, 0)

    shift[...] = jnp.transpose(jnp.broadcast_to(bias[...], (L, channels)))
    fetch.wait()

    def weigh(k, carry):
        high, low = split(wf[k])
        wh[:, pl.ds(pl.multiple_of(k * channels, channels), channels)] = high
        wl[:, pl.ds(pl.multiple_of(k * channels, channels), channels)] = low
        return carry

    lax.fori_loop(0, K, weigh, 0)

    own.wait()
    for r in range(ROWS):
        for dst in (r, 2 * ROWS + r):
            send(r, dst, r, east).wait_recv()

    def choose(s):
        for t in range(TAPS):
            high, low = split(ext[rows[s] + ROWS + taps[rows[s], t]])
            xs[s, :, pl.ds(L * t, L)] = high
            xs[s, :, pl.ds(L * (TAPS + t), L)] = high
            xs[s, :, pl.ds(L * (2 * TAPS + t), L)] = low

    def correlate(s, table):
        bands = jnp.concatenate([table[...], table[:, : TAPS * L]], axis=1)
        return split(product(bands, xs[s]))

    def mix(high, low):
        return product(
            jnp.concatenate([wh[...], wh[...], wl[...]], axis=1), jnp.concatenate([high, low, high], axis=1)
        )

    def correlate_sides(s):
        h = HALO[s]
        for part, value in enumerate(correlate(s, beside[s])):
            for k in range(K):
                for side in range(2):
                    sides[part, GROUP[s], pl.ds(L * side + BASE[s], h), pl.ds(channels * k, channels)] = value[
                        (2 * k + side) * h : (2 * k + side + 1) * h
                    ]

    def correlate_centre(s):
        for part, value in enumerate(correlate(s, centre.at[s])):
            for k in range(K):
                middle[part, pl.ds(L * s, L), pl.ds(channels * k, channels)] = value[k * L : (k + 1) * L]

    def halo(side, group):
        return pltpu.make_async_remote_copy(
            src_ref=hsend.at[group, side], dst_ref=hrecv.at[group, side], send_sem=hsend_sem.at[group, side],
            recv_sem=hrecv_sem.at[group, side], device_id=(west, east)[side], device_id_type=MESH,
        )

    def hand_over(group):
        value = mix(sides[0, group], sides[1, group])
        for side in range(2):
            hsend[group, side] = value[:, L * side : L * (side + 1)]
            halo(side, group).start()

    choose(0)
    correlate_sides(0)
    hand_over(0)
    for s in range(1, ROWS):
        choose(s)
        correlate_sides(s)
    hand_over(1)
    for s in range(ROWS):
        correlate_centre(s)
    value = mix(middle[0], middle[1])

    for group in range(2):
        for side in range(2):
            halo(side, group).wait_recv()
    lane = lax.broadcasted_iota(jnp.int32, (channels, L), 1)
    for s in range(ROWS):
        h = HALO[s]
        total = value[:, L * s : L * (s + 1)] + shift[...]
        if h == L:
            total = total + hrecv[0, 0] + hrecv[0, 1]
        else:
            last_columns = pltpu.roll(hrecv[1, 0], L - h - BASE[s], 1)
            first_columns = hrecv[1, 1] if BASE[s] == 0 else pltpu.roll(hrecv[1, 1], L - BASE[s], 1)
            total = total + jnp.where(lane >= L - h, last_columns, 0.0) + jnp.where(lane < h, first_columns, 0.0)
        out[rows[s]] = total

    for r in range(ROWS):
        send(r, r, r, east).wait_send()
        send(r, r, ROWS + r, east).wait_send()
    for group in range(2):
        for side in range(2):
            halo(side, group).wait_send()


def per_device(lats, lons, features, basis_panels, weights, bias_term, widths, tap_rows):
    channels = features.shape[1]
    bf16, f32 = jnp.bfloat16, jnp.float32
    vmem, anywhere = pl.BlockSpec(memory_space=pltpu.VMEM), pl.BlockSpec(memory_space=pl.ANY)
    return pl.pallas_call(
        functools.partial(kernel, lats, lons),
        out_shape=jax.ShapeDtypeStruct(features.shape, f32),
        in_specs=[anywhere] * 6,
        out_specs=vmem,
        scratch_shapes=[
            pltpu.SMEM(widths.shape, jnp.int32),
            pltpu.SMEM(tap_rows.shape, jnp.int32),
            pltpu.VMEM((1, channels), f32),
            pltpu.VMEM((TAPS, K, ROWS, SPAN), f32),
            pltpu.VMEM((3 * ROWS, channels, L), f32),
            pltpu.VMEM(weights.shape, f32),
            pltpu.VMEM((channels, K * channels), bf16),
            pltpu.VMEM((channels, K * channels), bf16),
            pltpu.VMEM((TAPS * K, ROWS, 2 * L), f32),
            pltpu.VMEM((TAPS * K, ROWS, 2 * L), f32),
            *(pltpu.VMEM((K * 2 * h, 2 * TAPS * L), bf16) for h in HALO),
            pltpu.VMEM((ROWS, K * L, 2 * TAPS * L), bf16),
            pltpu.VMEM((ROWS, channels, 3 * TAPS * L), bf16),
            pltpu.VMEM((2, 2, 2 * L, K * channels), bf16),
            pltpu.VMEM((2, ROWS * L, K * channels), bf16),
            pltpu.VMEM((channels, L), f32),
            pltpu.VMEM((2, 2, channels, L), f32),
            pltpu.VMEM((2, 2, channels, L), f32),
            pltpu.SemaphoreType.DMA((2 * ROWS,)),
            pltpu.SemaphoreType.DMA((3 * ROWS,)),
            pltpu.SemaphoreType.DMA((2, 2)),
            pltpu.SemaphoreType.DMA((2, 2)),
            pltpu.SemaphoreType.DMA,
            pltpu.SemaphoreType.DMA,
            pltpu.SemaphoreType.DMA((4,)),
        ],
        compiler_params=pltpu.CompilerParams(
            collective_id=0, has_side_effects=True, vmem_limit_bytes=60 << 20
        ),
    )(widths, tap_rows, bias_term[None, :], jnp.transpose(basis_panels, (1, 2, 0, 3)), features, weights)


def solution(mesh):
    return jax.shard_map(
        functools.partial(per_device, mesh.shape["lat"], mesh.shape["lon"]),
        mesh=mesh,
        in_specs=(
            P("lat", None, "lon"),
            P("lat", None, None, None),
            P(),
            P(),
            P("lat"),
            P("lat", None),
        ),
        out_specs=P("lat", None, "lon"),
        check_vma=False,
    )
```

```python
import functools

import jax
import jax.numpy as jnp
from jax import lax
from jax.experimental import pallas as pl
from jax.experimental.pallas import tpu as pltpu
from jax.sharding import PartitionSpec as P

ROWS = 4
TAPS = 3
K = 9
SPAN = 255
WMAX = 127
L = 128
NEAR = (24, 48, 32, 24)
START = (0, 80, 48, 24)
SIDES = 2 * L
CENTRES = 5 * L
WIDE = 9 * L
MESH = pl.DeviceIdType.MESH


def split(x):
    high = x.astype(jnp.bfloat16)
    low = (x - high.astype(jnp.float32)).astype(jnp.bfloat16)
    return high, low


def product(a, b):
    return jnp.dot(a, b, preferred_element_type=jnp.float32)


def kernel(
    lats, lons,
    widths_in, taps_in, bias_in, basis_in, feat, weights,
    out,
    widths, taps, bias, basis, ext0, ext1, wf, wh, wl, panel, bands, t0, t1, t2, t3, xs, cr, acc, shift, hsend, hrecv,
    send_sem, recv_sem, hsend_sem, hrecv_sem, own_sem, w_sem, small_sem,
):
    la, lo = lax.axis_index("lat"), lax.axis_index("lon")
    channels, ext = feat.shape[1], (ext0, ext1)
    east = {"lat": la, "lon": lax.rem(lo + 1, lons)}
    west = {"lat": la, "lon": lax.rem(lo + lons - 1, lons)}
    half = {"lat": la, "lon": lax.rem(lo + lons // 2, lons)}
    above = {"lat": lax.rem(la + lats - 1, lats), "lon": lo}
    below = {"lat": lax.rem(la + 1, lats), "lon": lo}
    first, last = la == 0, la == lats - 1

    barrier = pltpu.get_barrier_semaphore()

    def greet(peer):
        pl.semaphore_signal(barrier, inc=1, device_id=peer, device_id_type=MESH)

    greet(east)
    greet(west)

    @pl.when(first)
    def _():
        greet(half)

    @pl.when(jnp.logical_not(first))
    def _():
        greet(above)

    @pl.when(last)
    def _():
        greet(half)

    @pl.when(jnp.logical_not(last))
    def _():
        greet(below)

    small = [
        pltpu.make_async_copy(src, dst, small_sem.at[i])
        for i, (src, dst) in enumerate(((widths_in, widths), (taps_in, taps), (bias_in, bias), (basis_in, basis)))
    ]
    part = channels // 2
    own = [
        pltpu.make_async_copy(feat.at[:, pl.ds(part * q, part)], ext[q].at[pl.ds(ROWS, ROWS)], own_sem.at[q])
        for q in range(2)
    ]
    fetch = pltpu.make_async_copy(weights, wf, w_sem)
    for copy in (*small, *own, fetch):
        copy.start()
    pl.semaphore_wait(barrier, 4)

    def send(src, dst, q, place, peer):
        some = pl.ds(part * q, part)
        return pltpu.make_async_remote_copy(
            src_ref=feat.at[src, some], dst_ref=ext[q].at[dst], send_sem=send_sem.at[q, place],
            recv_sem=recv_sem.at[q, dst], device_id=peer, device_id_type=MESH,
        )

    for q in range(2):

        @pl.when(first)
        def _(q=q):
            for r in range(ROWS):
                send(r, ROWS - 1 - r, q, r, half).start()

        @pl.when(last)
        def _(q=q):
            for r in range(ROWS):
                send(r, 3 * ROWS - 1 - r, q, ROWS + r, half).start()

        @pl.when(jnp.logical_not(first))
        def _(q=q):
            for r in range(ROWS):
                send(r, 2 * ROWS + r, q, r, above).start()

        @pl.when(jnp.logical_not(last))
        def _(q=q):
            for r in range(ROWS):
                send(r, r, q, ROWS + r, below).start()

    flip = la // (lats // 2)
    rows = [s + flip * (ROWS - 1 - 2 * s) for s in range(ROWS)]

    for copy in small:
        copy.wait()
    row = lax.broadcasted_iota(jnp.int32, (ROWS, SPAN), 0)
    limit = jnp.full((ROWS, SPAN), widths[0])
    for r in range(1, ROWS):
        limit = jnp.where(row == r, widths[r], limit)
    inside = jnp.abs(lax.broadcasted_iota(jnp.int32, (ROWS, SPAN), 1) - WMAX) <= limit
    panel[...] = jnp.zeros_like(panel)
    for t in range(TAPS):
        for k in range(K):
            panel[pl.ds(ROWS * (K * t + k), ROWS), pl.ds(0, SPAN)] = jnp.where(inside, basis[t, k], 0.0)
    source = lax.broadcasted_iota(jnp.int32, (2 * L, 2 * L), 0)
    target = lax.broadcasted_iota(jnp.int32, (2 * L, 2 * L), 1)
    back = WMAX - target
    back = jnp.where(back < -1, back + 2 * L, back)
    move = jnp.where(source == back, 1.0, 0.0).astype(jnp.bfloat16)
    high, low = split(panel[...])
    bands[...] = product(high, move) + product(low, move)

    line = lax.broadcasted_iota(jnp.int32, (L, L), 0)
    lane = lax.broadcasted_iota(jnp.int32, (L, L), 1)
    tables = (t0, t1, t2, t3)
    outer = [2 * L, L, L, L]

    for s in range(ROWS):

        def fill(k, carry, s=s, table=tables[s], width=outer[s]):
            for t in range(TAPS):
                band = jnp.broadcast_to(bands[pl.ds(ROWS * (K * t + k) + rows[s], 1), :], (L, 2 * L))
                band = pltpu.roll(band, 0, 1, stride=1, stride_axis=0)
                inner, side = band[:, :L], band[:, L:]
                if width == 2 * L:
                    side = jnp.concatenate(
                        [jnp.where(line < lane, side, 0.0), jnp.where(line > lane, side, 0.0)], axis=1
                    )
                for at, value in ((k * width, side), (K * width + k * L, inner)):
                    spot = pl.ds(pl.multiple_of(at, L), value.shape[1])
                    for p, piece in enumerate(split(value)):
                        table[pl.ds(L * (TAPS * p + t), L), spot] = piece
            return carry

        lax.fori_loop(0, K, fill, 0)

    shift[...] = jnp.transpose(jnp.broadcast_to(bias[...], (L, channels)))
    fetch.wait()

    def weigh(k, carry):
        spot = pl.ds(pl.multiple_of(k * part, part), part)
        high, low = split(wf[k])
        for q in range(2):
            wh[q, :, spot] = high[:, part * q : part * (q + 1)]
            wl[q, :, spot] = low[:, part * q : part * (q + 1)]
        return carry

    lax.fori_loop(0, K, weigh, 0)
    for copy in own:
        copy.wait()

    def choose(q, s):
        for t in range(TAPS):
            high, low = split(ext[q][rows[s] + ROWS + taps[rows[s], t]])
            xs[q, s, :, pl.ds(L * t, L)] = high
            xs[q, s, :, pl.ds(L * (TAPS + t), L)] = high
            xs[q, s, :, pl.ds(L * (2 * TAPS + t), L)] = low

    def correlate(q, s, start, width, at):
        size = K * width
        table = tables[s]
        bands = jnp.concatenate([table[:, start : start + size], table[: TAPS * L, start : start + size]], axis=0)
        for p, value in enumerate(split(product(xs[q, s], bands))):
            for k in range(K):
                cr[p, q, pl.ds(part * k, part), pl.ds(at, width)] = value[:, width * k : width * (k + 1)]

    def correlate_sides(q, s):
        correlate(q, s, 0, outer[s], 0 if s == 0 else SIDES + L * (s - 1))

    def correlate_centre(q, s):
        correlate(q, s, K * outer[s], L, CENTRES + L * s)

    def mix(q, start, stop):
        high, low = cr[0, q, :, start:stop], cr[1, q, :, start:stop]
        return product(
            jnp.concatenate([wh[q], wh[q], wl[q]], axis=1), jnp.concatenate([high, low, high], axis=0)
        )

    def halo(side, group):
        return pltpu.make_async_remote_copy(
            src_ref=hsend.at[group, side], dst_ref=hrecv.at[group, side], send_sem=hsend_sem.at[group, side],
            recv_sem=hrecv_sem.at[group, side], device_id=(west, east)[side], device_id_type=MESH,
        )

    def arrive(q):
        for r in range(ROWS):
            for dst in (r, 2 * ROWS + r):
                send(r, dst, q, r, east).wait_recv()

    arrive(0)
    for s in range(ROWS):
        choose(0, s)
        correlate_sides(0, s)
        correlate_centre(0, s)
    acc[...] = mix(0, 0, WIDE)

    arrive(1)
    pole = jnp.logical_or(first, last)
    choose(1, 0)
    correlate_sides(1, 0)
    wide = mix(1, 0, SIDES) + acc[:, :SIDES]
    hsend[0, 0] = wide[:, :L]
    hsend[0, 1] = wide[:, L:]

    @pl.when(pole)
    def _():
        for side in range(2):
            halo(side, 0).start()

    for s in range(1, ROWS):
        choose(1, s)
        correlate_sides(1, s)
    value = mix(1, SIDES, CENTRES) + acc[:, SIDES:CENTRES]
    lane = lax.broadcasted_iota(jnp.int32, (channels, L), 1)
    for side in range(2):
        packed = jnp.zeros((channels, L), jnp.float32)
        for s in range(ROWS):
            block = hsend[0, side] if s == 0 else value[:, L * (s - 1) : L * s]
            by = (START[s] - (L - NEAR[s] if side == 0 else 0)) % L
            block = pltpu.roll(block, by, 1) if by else block
            packed = jnp.where((lane >= START[s]) & (lane < START[s] + NEAR[s]), block, packed)
        hsend[1, side] = packed
        halo(side, 1).start()
    for s in range(ROWS):
        correlate_centre(1, s)
    value = mix(1, CENTRES, WIDE) + acc[:, CENTRES:]

    @pl.when(pole)
    def _():
        for side in range(2):
            halo(side, 0).wait_recv()

    for side in range(2):
        halo(side, 1).wait_recv()
    for s in range(ROWS):
        total = value[:, L * s : L * (s + 1)] + shift[...]
        for side in range(2):
            by = ((L - NEAR[s] if side == 0 else 0) - START[s]) % L
            block = pltpu.roll(hrecv[1, side], by, 1) if by else hrecv[1, side]
            near = (lane >= L - NEAR[s]) if side == 0 else (lane < NEAR[s])
            total = total + jnp.where(near, block, 0.0)
            if s == 0:
                total = total + jnp.where(jnp.logical_and(pole, jnp.logical_not(near)), hrecv[0, side], 0.0)
        out[rows[s]] = total

    for q in range(2):
        for r in range(ROWS):
            send(r, r, q, r, east).wait_send()
            send(r, r, q, ROWS + r, east).wait_send()

    @pl.when(pole)
    def _():
        for side in range(2):
            halo(side, 0).wait_send()

    for side in range(2):
        halo(side, 1).wait_send()


def per_device(lats, lons, features, basis_panels, weights, bias_term, widths, tap_rows):
    channels = features.shape[1]
    bf16, f32 = jnp.bfloat16, jnp.float32
    vmem, anywhere = pl.BlockSpec(memory_space=pltpu.VMEM), pl.BlockSpec(memory_space=pl.ANY)
    return pl.pallas_call(
        functools.partial(kernel, lats, lons),
        out_shape=jax.ShapeDtypeStruct(features.shape, f32),
        in_specs=[anywhere] * 6,
        out_specs=vmem,
        scratch_shapes=[
            pltpu.SMEM(widths.shape, jnp.int32),
            pltpu.SMEM(tap_rows.shape, jnp.int32),
            pltpu.VMEM((1, channels), f32),
            pltpu.VMEM((TAPS, K, ROWS, SPAN), f32),
            pltpu.VMEM((3 * ROWS, channels // 2, L), f32),
            pltpu.VMEM((3 * ROWS, channels // 2, L), f32),
            pltpu.VMEM(weights.shape, f32),
            pltpu.VMEM((2, channels, K * channels // 2), bf16),
            pltpu.VMEM((2, channels, K * channels // 2), bf16),
            pltpu.VMEM((TAPS * K * ROWS, 2 * L), f32),
            pltpu.VMEM((TAPS * K * ROWS, 2 * L), f32),
            *(pltpu.VMEM((2 * TAPS * L, K * n * L), bf16) for n in (3, 2, 2, 2)),
            pltpu.VMEM((2, ROWS, channels // 2, 3 * TAPS * L), bf16),
            pltpu.VMEM((2, 2, K * channels // 2, WIDE), bf16),
            pltpu.VMEM((channels, WIDE), f32),
            pltpu.VMEM((channels, L), f32),
            pltpu.VMEM((2, 2, channels, L), f32),
            pltpu.VMEM((2, 2, channels, L), f32),
            pltpu.SemaphoreType.DMA((2, 2 * ROWS)),
            pltpu.SemaphoreType.DMA((2, 3 * ROWS)),
            pltpu.SemaphoreType.DMA((2, 2)),
            pltpu.SemaphoreType.DMA((2, 2)),
            pltpu.SemaphoreType.DMA((2,)),
            pltpu.SemaphoreType.DMA,
            pltpu.SemaphoreType.DMA((4,)),
        ],
        compiler_params=pltpu.CompilerParams(
            collective_id=0, has_side_effects=True, vmem_limit_bytes=60 << 20
        ),
    )(widths, tap_rows, bias_term[None, :], jnp.transpose(basis_panels, (1, 2, 0, 3)), features, weights)


def solution(mesh):
    return jax.shard_map(
        functools.partial(per_device, mesh.shape["lat"], mesh.shape["lon"]),
        mesh=mesh,
        in_specs=(
            P("lat", None, "lon"),
            P("lat", None, None, None),
            P(),
            P(),
            P("lat"),
            P("lat", None),
        ),
        out_specs=P("lat", None, "lon"),
        check_vma=False,
    )
```

```python
import functools

import jax
import jax.numpy as jnp
from jax import lax
from jax.experimental import pallas as pl
from jax.experimental.pallas import tpu as pltpu
from jax.sharding import PartitionSpec as P

ROWS = 4
TAPS = 3
K = 9
SPAN = 255
WMAX = 127
L = 128
NEAR = (24, 48, 32, 24)
START = (0, 80, 48, 24)
SIDES = 2 * L
CENTRES = 5 * L
WIDE = 9 * L
EARLY = 2
MESH = pl.DeviceIdType.MESH


def split(x):
    high = x.astype(jnp.bfloat16)
    low = (x - high.astype(jnp.float32)).astype(jnp.bfloat16)
    return high, low


def product(a, b):
    return jnp.dot(a, b, preferred_element_type=jnp.float32)


def kernel(
    lats, lons,
    widths_in, taps_in, bias_in, basis_in, feat, weights,
    out,
    widths, taps, bias, basis, ext0, ext1, wf, wh, wl, panel, bands, t0, t1, t2, t3, xs, cr, acc, shift, hsend, hrecv,
    send_sem, recv_sem, hsend_sem, hrecv_sem, own_sem, w_sem, small_sem,
):
    la, lo = lax.axis_index("lat"), lax.axis_index("lon")
    channels, ext = feat.shape[1], (ext0, ext1)
    east = {"lat": la, "lon": lax.rem(lo + 1, lons)}
    west = {"lat": la, "lon": lax.rem(lo + lons - 1, lons)}
    half = {"lat": la, "lon": lax.rem(lo + lons // 2, lons)}
    above = {"lat": lax.rem(la + lats - 1, lats), "lon": lo}
    below = {"lat": lax.rem(la + 1, lats), "lon": lo}
    first, last = la == 0, la == lats - 1

    barrier = pltpu.get_barrier_semaphore()

    def greet(peer):
        pl.semaphore_signal(barrier, inc=1, device_id=peer, device_id_type=MESH)

    greet(east)
    greet(west)

    @pl.when(first)
    def _():
        greet(half)

    @pl.when(jnp.logical_not(first))
    def _():
        greet(above)

    @pl.when(last)
    def _():
        greet(half)

    @pl.when(jnp.logical_not(last))
    def _():
        greet(below)

    small = [
        pltpu.make_async_copy(src, dst, small_sem.at[i])
        for i, (src, dst) in enumerate(((widths_in, widths), (taps_in, taps), (bias_in, bias), (basis_in, basis)))
    ]
    part = channels // 2
    own = [
        pltpu.make_async_copy(feat.at[:, pl.ds(part * q, part)], ext[q].at[pl.ds(ROWS, ROWS)], own_sem.at[q])
        for q in range(2)
    ]
    fetch = pltpu.make_async_copy(weights, wf, w_sem)
    for copy in (*small, *own, fetch):
        copy.start()
    pl.semaphore_wait(barrier, 4)

    def send(src, dst, q, place, peer):
        some = pl.ds(part * q, part)
        return pltpu.make_async_remote_copy(
            src_ref=feat.at[src, some], dst_ref=ext[q].at[dst], send_sem=send_sem.at[q, place],
            recv_sem=recv_sem.at[q, dst], device_id=peer, device_id_type=MESH,
        )

    for q in range(2):

        @pl.when(first)
        def _(q=q):
            for r in range(ROWS):
                send(r, ROWS - 1 - r, q, r, half).start()

        @pl.when(last)
        def _(q=q):
            for r in range(ROWS):
                send(r, 3 * ROWS - 1 - r, q, ROWS + r, half).start()

        @pl.when(jnp.logical_not(first))
        def _(q=q):
            for r in range(ROWS):
                send(r, 2 * ROWS + r, q, r, above).start()

        @pl.when(jnp.logical_not(last))
        def _(q=q):
            for r in range(ROWS):
                send(r, r, q, ROWS + r, below).start()

    flip = la // (lats // 2)
    rows = [s + flip * (ROWS - 1 - 2 * s) for s in range(ROWS)]

    for copy in small:
        copy.wait()
    row = lax.broadcasted_iota(jnp.int32, (ROWS, SPAN), 0)
    limit = jnp.full((ROWS, SPAN), widths[0])
    for r in range(1, ROWS):
        limit = jnp.where(row == r, widths[r], limit)
    inside = jnp.abs(lax.broadcasted_iota(jnp.int32, (ROWS, SPAN), 1) - WMAX) <= limit
    panel[...] = jnp.zeros_like(panel)
    for t in range(TAPS):
        for k in range(K):
            panel[pl.ds(ROWS * (K * t + k), ROWS), pl.ds(0, SPAN)] = jnp.where(inside, basis[t, k], 0.0)
    source = lax.broadcasted_iota(jnp.int32, (2 * L, 2 * L), 0)
    target = lax.broadcasted_iota(jnp.int32, (2 * L, 2 * L), 1)
    back = WMAX - target
    back = jnp.where(back < -1, back + 2 * L, back)
    move = jnp.where(source == back, 1.0, 0.0).astype(jnp.bfloat16)
    high, low = split(panel[...])
    bands[...] = product(high, move) + product(low, move)

    line = lax.broadcasted_iota(jnp.int32, (L, L), 0)
    lane = lax.broadcasted_iota(jnp.int32, (L, L), 1)
    tables = (t0, t1, t2, t3)
    outer = [2 * L, L, L, L]

    for s in range(ROWS):

        def fill(k, carry, s=s, table=tables[s], width=outer[s]):
            for t in range(TAPS):
                band = jnp.broadcast_to(bands[pl.ds(ROWS * (K * t + k) + rows[s], 1), :], (L, 2 * L))
                band = pltpu.roll(band, 0, 1, stride=1, stride_axis=0)
                inner, side = band[:, :L], band[:, L:]
                if width == 2 * L:
                    side = jnp.concatenate(
                        [jnp.where(line < lane, side, 0.0), jnp.where(line > lane, side, 0.0)], axis=1
                    )
                for at, value in ((k * width, side), (K * width + k * L, inner)):
                    spot = pl.ds(pl.multiple_of(at, L), value.shape[1])
                    for p, piece in enumerate(split(value)):
                        table[pl.ds(L * (TAPS * p + t), L), spot] = piece
            return carry

        lax.fori_loop(0, K, fill, 0)

    shift[...] = jnp.transpose(jnp.broadcast_to(bias[...], (L, channels)))
    fetch.wait()

    def weigh(k, carry):
        spot = pl.ds(pl.multiple_of(k * part, part), part)
        high, low = split(wf[k])
        for q in range(2):
            wh[q, :, spot] = high[:, part * q : part * (q + 1)]
            wl[q, :, spot] = low[:, part * q : part * (q + 1)]
        return carry

    lax.fori_loop(0, K, weigh, 0)
    for copy in own:
        copy.wait()

    def choose(q, s):
        for t in range(TAPS):
            high, low = split(ext[q][rows[s] + ROWS + taps[rows[s], t]])
            xs[q, s, :, pl.ds(L * t, L)] = high
            xs[q, s, :, pl.ds(L * (TAPS + t), L)] = high
            xs[q, s, :, pl.ds(L * (2 * TAPS + t), L)] = low

    def correlate(q, s, start, width, at):
        size = K * width
        table = tables[s]
        bands = jnp.concatenate([table[:, start : start + size], table[: TAPS * L, start : start + size]], axis=0)
        for p, value in enumerate(split(product(xs[q, s], bands))):
            for k in range(K):
                cr[p, q, pl.ds(part * k, part), pl.ds(at, width)] = value[:, width * k : width * (k + 1)]

    def correlate_sides(q, s):
        correlate(q, s, 0, outer[s], 0 if s == 0 else SIDES + L * (s - 1))

    def correlate_centre(q, s):
        correlate(q, s, K * outer[s], L, CENTRES + L * s)

    def mix(q, start, stop):
        high, low = cr[0, q, :, start:stop], cr[1, q, :, start:stop]
        return product(
            jnp.concatenate([wh[q], wh[q], wl[q]], axis=1), jnp.concatenate([high, low, high], axis=0)
        )

    def halo(side, group):
        return pltpu.make_async_remote_copy(
            src_ref=hsend.at[group, side], dst_ref=hrecv.at[group, side], send_sem=hsend_sem.at[group, side],
            recv_sem=hrecv_sem.at[group, side], device_id=(west, east)[side], device_id_type=MESH,
        )

    def arrive(q):
        for r in range(ROWS):
            for dst in (r, 2 * ROWS + r):
                send(r, dst, q, r, east).wait_recv()

    arrive(0)
    for s in range(ROWS):
        choose(0, s)
        correlate_sides(0, s)
    acc[...] = mix(0, 0, CENTRES)
    for s in range(EARLY):
        correlate_centre(0, s)

    arrive(1)
    pole = jnp.logical_or(first, last)
    choose(1, 0)
    correlate_sides(1, 0)
    wide = mix(1, 0, SIDES) + acc[:, :SIDES]
    hsend[0, 0] = wide[:, :L]
    hsend[0, 1] = wide[:, L:]

    @pl.when(pole)
    def _():
        for side in range(2):
            halo(side, 0).start()

    for s in range(1, ROWS):
        choose(1, s)
        correlate_sides(1, s)
    value = mix(1, SIDES, CENTRES) + acc[:, SIDES:]
    lane = lax.broadcasted_iota(jnp.int32, (channels, L), 1)
    for side in range(2):
        packed = jnp.zeros((channels, L), jnp.float32)
        for s in range(ROWS):
            block = hsend[0, side] if s == 0 else value[:, L * (s - 1) : L * s]
            by = (START[s] - (L - NEAR[s] if side == 0 else 0)) % L
            block = pltpu.roll(block, by, 1) if by else block
            packed = jnp.where((lane >= START[s]) & (lane < START[s] + NEAR[s]), block, packed)
        hsend[1, side] = packed
        halo(side, 1).start()
    for s in range(ROWS):
        if s >= EARLY:
            correlate_centre(0, s)
        correlate_centre(1, s)
    value = mix(0, CENTRES, WIDE) + mix(1, CENTRES, WIDE)

    @pl.when(pole)
    def _():
        for side in range(2):
            halo(side, 0).wait_recv()

    for side in range(2):
        halo(side, 1).wait_recv()
    for s in range(ROWS):
        total = value[:, L * s : L * (s + 1)] + shift[...]
        for side in range(2):
            by = ((L - NEAR[s] if side == 0 else 0) - START[s]) % L
            block = pltpu.roll(hrecv[1, side], by, 1) if by else hrecv[1, side]
            near = (lane >= L - NEAR[s]) if side == 0 else (lane < NEAR[s])
            total = total + jnp.where(near, block, 0.0)
            if s == 0:
                total = total + jnp.where(jnp.logical_and(pole, jnp.logical_not(near)), hrecv[0, side], 0.0)
        out[rows[s]] = total

    for q in range(2):
        for r in range(ROWS):
            send(r, r, q, r, east).wait_send()
            send(r, r, q, ROWS + r, east).wait_send()

    @pl.when(pole)
    def _():
        for side in range(2):
            halo(side, 0).wait_send()

    for side in range(2):
        halo(side, 1).wait_send()


def per_device(lats, lons, features, basis_panels, weights, bias_term, widths, tap_rows):
    channels = features.shape[1]
    bf16, f32 = jnp.bfloat16, jnp.float32
    vmem, anywhere = pl.BlockSpec(memory_space=pltpu.VMEM), pl.BlockSpec(memory_space=pl.ANY)
    return pl.pallas_call(
        functools.partial(kernel, lats, lons),
        out_shape=jax.ShapeDtypeStruct(features.shape, f32),
        in_specs=[anywhere] * 6,
        out_specs=vmem,
        scratch_shapes=[
            pltpu.SMEM(widths.shape, jnp.int32),
            pltpu.SMEM(tap_rows.shape, jnp.int32),
            pltpu.VMEM((1, channels), f32),
            pltpu.VMEM((TAPS, K, ROWS, SPAN), f32),
            pltpu.VMEM((3 * ROWS, channels // 2, L), f32),
            pltpu.VMEM((3 * ROWS, channels // 2, L), f32),
            pltpu.VMEM(weights.shape, f32),
            pltpu.VMEM((2, channels, K * channels // 2), bf16),
            pltpu.VMEM((2, channels, K * channels // 2), bf16),
            pltpu.VMEM((TAPS * K * ROWS, 2 * L), f32),
            pltpu.VMEM((TAPS * K * ROWS, 2 * L), f32),
            *(pltpu.VMEM((2 * TAPS * L, K * n * L), bf16) for n in (3, 2, 2, 2)),
            pltpu.VMEM((2, ROWS, channels // 2, 3 * TAPS * L), bf16),
            pltpu.VMEM((2, 2, K * channels // 2, WIDE), bf16),
            pltpu.VMEM((channels, CENTRES), f32),
            pltpu.VMEM((channels, L), f32),
            pltpu.VMEM((2, 2, channels, L), f32),
            pltpu.VMEM((2, 2, channels, L), f32),
            pltpu.SemaphoreType.DMA((2, 2 * ROWS)),
            pltpu.SemaphoreType.DMA((2, 3 * ROWS)),
            pltpu.SemaphoreType.DMA((2, 2)),
            pltpu.SemaphoreType.DMA((2, 2)),
            pltpu.SemaphoreType.DMA((2,)),
            pltpu.SemaphoreType.DMA,
            pltpu.SemaphoreType.DMA((4,)),
        ],
        compiler_params=pltpu.CompilerParams(
            collective_id=0, has_side_effects=True, vmem_limit_bytes=60 << 20
        ),
    )(widths, tap_rows, bias_term[None, :], jnp.transpose(basis_panels, (1, 2, 0, 3)), features, weights)


def solution(mesh):
    return jax.shard_map(
        functools.partial(per_device, mesh.shape["lat"], mesh.shape["lon"]),
        mesh=mesh,
        in_specs=(
            P("lat", None, "lon"),
            P("lat", None, None, None),
            P(),
            P(),
            P("lat"),
            P("lat", None),
        ),
        out_specs=P("lat", None, "lon"),
        check_vma=False,
    )
```

```python
import functools

import jax
import jax.numpy as jnp
from jax import lax
from jax.experimental import pallas as pl
from jax.experimental.pallas import tpu as pltpu
from jax.sharding import PartitionSpec as P

ROWS = 4
TAPS = 3
K = 9
SPAN = 255
WMAX = 127
L = 128
NEAR = (24, 48, 32, 24)
START = (0, 80, 48, 24)
SIDES = 2 * L
CENTRES = 5 * L
WIDE = 9 * L
EARLY = 2
MESH = pl.DeviceIdType.MESH


def split(x):
    high = x.astype(jnp.bfloat16)
    low = (x - high.astype(jnp.float32)).astype(jnp.bfloat16)
    return high, low


def product(a, b):
    return jnp.dot(a, b, preferred_element_type=jnp.float32)


def kernel(
    lats, lons,
    widths_in, taps_in, bias_in, basis_in, feat, weights,
    out,
    widths, taps, bias, basis, ext0, ext1, wf, wh, wl, panel, bands, t0, t1, t2, t3, xs, cr, acc, shift, hsend, hrecv,
    send_sem, recv_sem, hsend_sem, hrecv_sem, own_sem, w_sem, small_sem,
):
    la, lo = lax.axis_index("lat"), lax.axis_index("lon")
    channels, ext = feat.shape[1], (ext0, ext1)
    east = {"lat": la, "lon": lax.rem(lo + 1, lons)}
    west = {"lat": la, "lon": lax.rem(lo + lons - 1, lons)}
    half = {"lat": la, "lon": lax.rem(lo + lons // 2, lons)}
    above = {"lat": lax.rem(la + lats - 1, lats), "lon": lo}
    below = {"lat": lax.rem(la + 1, lats), "lon": lo}
    first, last = la == 0, la == lats - 1

    barrier = pltpu.get_barrier_semaphore()

    def greet(peer):
        pl.semaphore_signal(barrier, inc=1, device_id=peer, device_id_type=MESH)

    greet(east)
    greet(west)

    @pl.when(first)
    def _():
        greet(half)

    @pl.when(jnp.logical_not(first))
    def _():
        greet(above)

    @pl.when(last)
    def _():
        greet(half)

    @pl.when(jnp.logical_not(last))
    def _():
        greet(below)

    small = [
        pltpu.make_async_copy(src, dst, small_sem.at[i])
        for i, (src, dst) in enumerate(((widths_in, widths), (taps_in, taps), (bias_in, bias), (basis_in, basis)))
    ]
    part = channels // 2
    own = [
        pltpu.make_async_copy(feat.at[:, pl.ds(part * q, part)], ext[q].at[pl.ds(ROWS, ROWS)], own_sem.at[q])
        for q in range(2)
    ]
    fetch = pltpu.make_async_copy(weights, wf, w_sem)
    for copy in (*small, *own, fetch):
        copy.start()
    pl.semaphore_wait(barrier, 4)

    def send(src, dst, q, place, peer):
        some = pl.ds(part * q, part)
        return pltpu.make_async_remote_copy(
            src_ref=feat.at[src, some], dst_ref=ext[q].at[dst], send_sem=send_sem.at[q, place],
            recv_sem=recv_sem.at[q, dst], device_id=peer, device_id_type=MESH,
        )

    for q in range(2):

        @pl.when(first)
        def _(q=q):
            for r in range(ROWS):
                send(r, ROWS - 1 - r, q, r, half).start()

        @pl.when(last)
        def _(q=q):
            for r in range(ROWS):
                send(r, 3 * ROWS - 1 - r, q, ROWS + r, half).start()

        @pl.when(jnp.logical_not(first))
        def _(q=q):
            for r in range(ROWS):
                send(r, 2 * ROWS + r, q, r, above).start()

        @pl.when(jnp.logical_not(last))
        def _(q=q):
            for r in range(ROWS):
                send(r, r, q, ROWS + r, below).start()

    flip = la // (lats // 2)
    rows = [s + flip * (ROWS - 1 - 2 * s) for s in range(ROWS)]

    for copy in small:
        copy.wait()
    row = lax.broadcasted_iota(jnp.int32, (ROWS, SPAN), 0)
    limit = jnp.full((ROWS, SPAN), widths[0])
    for r in range(1, ROWS):
        limit = jnp.where(row == r, widths[r], limit)
    inside = jnp.abs(lax.broadcasted_iota(jnp.int32, (ROWS, SPAN), 1) - WMAX) <= limit
    panel[...] = jnp.zeros_like(panel)
    for t in range(TAPS):
        for k in range(K):
            panel[pl.ds(ROWS * (K * t + k), ROWS), pl.ds(0, SPAN)] = jnp.where(inside, basis[t, k], 0.0)
    source = lax.broadcasted_iota(jnp.int32, (2 * L, 2 * L), 0)
    target = lax.broadcasted_iota(jnp.int32, (2 * L, 2 * L), 1)
    back = WMAX - target
    back = jnp.where(back < -1, back + 2 * L, back)
    move = jnp.where(source == back, 1.0, 0.0).astype(jnp.bfloat16)
    high, low = split(panel[...])
    bands[...] = product(high, move) + product(low, move)

    line = lax.broadcasted_iota(jnp.int32, (L, L), 0)
    lane = lax.broadcasted_iota(jnp.int32, (L, L), 1)
    tables = (t0, t1, t2, t3)
    outer = [2 * L, L, L, L]

    for s in range(ROWS):

        def fill(k, carry, s=s, table=tables[s], width=outer[s]):
            for t in range(TAPS):
                band = jnp.broadcast_to(bands[pl.ds(ROWS * (K * t + k) + rows[s], 1), :], (L, 2 * L))
                band = pltpu.roll(band, 0, 1, stride=1, stride_axis=0)
                inner, side = band[:, :L], band[:, L:]
                if width == 2 * L:
                    side = jnp.concatenate(
                        [jnp.where(line < lane, side, 0.0), jnp.where(line > lane, side, 0.0)], axis=1
                    )
                for at, value in ((k * width, side), (K * width + k * L, inner)):
                    spot = pl.ds(pl.multiple_of(at, L), value.shape[1])
                    for p, piece in enumerate(split(value)):
                        table[pl.ds(L * (TAPS * p + t), L), spot] = piece
            return carry

        lax.fori_loop(0, K, fill, 0)

    shift[...] = jnp.transpose(jnp.broadcast_to(bias[...], (L, channels)))
    fetch.wait()

    def weigh(k, carry):
        spot = pl.ds(pl.multiple_of(k * part, part), part)
        high, low = split(wf[k])
        for q in range(2):
            wh[q, :, spot] = high[:, part * q : part * (q + 1)]
            wl[q, :, spot] = low[:, part * q : part * (q + 1)]
        return carry

    lax.fori_loop(0, K, weigh, 0)
    for copy in own:
        copy.wait()

    def choose(q, s):
        for t in range(TAPS):
            high, low = split(ext[q][rows[s] + ROWS + taps[rows[s], t]])
            xs[q, s, :, pl.ds(L * t, L)] = high
            xs[q, s, :, pl.ds(L * (TAPS + t), L)] = high
            xs[q, s, :, pl.ds(L * (2 * TAPS + t), L)] = low

    def correlate(q, s, start, width, at):
        size = K * width
        table = tables[s]
        bands = jnp.concatenate([table[:, start : start + size], table[: TAPS * L, start : start + size]], axis=0)
        for p, value in enumerate(split(product(xs[q, s], bands))):
            for k in range(K):
                cr[p, q, pl.ds(part * k, part), pl.ds(at, width)] = value[:, width * k : width * (k + 1)]

    def correlate_sides(q, s):
        correlate(q, s, 0, outer[s], 0 if s == 0 else SIDES + L * (s - 1))

    def correlate_centre(q, s):
        correlate(q, s, K * outer[s], L, CENTRES + L * s)

    def mix(q, start, stop):
        high, low = cr[0, q, :, start:stop], cr[1, q, :, start:stop]
        return product(
            jnp.concatenate([wh[q], wh[q], wl[q]], axis=1), jnp.concatenate([high, low, high], axis=0)
        )

    def halo(side, group):
        return pltpu.make_async_remote_copy(
            src_ref=hsend.at[group, side], dst_ref=hrecv.at[group, side], send_sem=hsend_sem.at[group, side],
            recv_sem=hrecv_sem.at[group, side], device_id=(west, east)[side], device_id_type=MESH,
        )

    def arrive(q):
        for r in range(ROWS):
            for dst in (r, 2 * ROWS + r):
                send(r, dst, q, r, east).wait_recv()

    arrive(0)
    for s in range(ROWS):
        choose(0, s)
        correlate_sides(0, s)
    acc[...] = mix(0, 0, CENTRES)
    for s in range(EARLY):
        correlate_centre(0, s)

    arrive(1)
    pole = jnp.logical_or(first, last)
    choose(1, 0)
    correlate_sides(1, 0)
    wide = mix(1, 0, SIDES) + acc[:, :SIDES]
    hsend[0, 0] = wide[:, :L]
    hsend[0, 1] = wide[:, L:]

    @pl.when(pole)
    def _():
        for side in range(2):
            halo(side, 0).start()

    for s in range(1, ROWS):
        choose(1, s)
        correlate_sides(1, s)
    value = mix(1, SIDES, CENTRES) + acc[:, SIDES:]
    lane = lax.broadcasted_iota(jnp.int32, (channels, L), 1)
    for side in range(2):
        packed = jnp.zeros((channels, L), jnp.float32)
        for s in range(ROWS):
            block = hsend[0, side] if s == 0 else value[:, L * (s - 1) : L * s]
            by = (START[s] - (L - NEAR[s] if side == 0 else 0)) % L
            block = pltpu.roll(block, by, 1) if by else block
            packed = jnp.where((lane >= START[s]) & (lane < START[s] + NEAR[s]), block, packed)
        hsend[1, side] = packed
        halo(side, 1).start()
    for s in range(ROWS):
        if s >= EARLY:
            correlate_centre(0, s)
        correlate_centre(1, s)
    value = mix(0, CENTRES, WIDE) + mix(1, CENTRES, WIDE)

    @pl.when(pole)
    def _():
        for side in range(2):
            halo(side, 0).wait_recv()

    for side in range(2):
        halo(side, 1).wait_recv()
    for s in range(ROWS):
        total = value[:, L * s : L * (s + 1)] + shift[...]
        for side in range(2):
            by = ((L - NEAR[s] if side == 0 else 0) - START[s]) % L
            block = pltpu.roll(hrecv[1, side], by, 1) if by else hrecv[1, side]
            near = (lane >= L - NEAR[s]) if side == 0 else (lane < NEAR[s])
            total = total + jnp.where(near, block, 0.0)
            if s == 0:
                total = total + jnp.where(jnp.logical_and(pole, jnp.logical_not(near)), hrecv[0, side], 0.0)
        out[rows[s]] = total

    for q in range(2):
        for r in range(ROWS):
            send(r, r, q, r, east).wait_send()
            send(r, r, q, ROWS + r, east).wait_send()

    @pl.when(pole)
    def _():
        for side in range(2):
            halo(side, 0).wait_send()

    for side in range(2):
        halo(side, 1).wait_send()


def per_device(lats, lons, features, basis_panels, weights, bias_term, widths, tap_rows):
    channels = features.shape[1]
    bf16, f32 = jnp.bfloat16, jnp.float32
    vmem, anywhere = pl.BlockSpec(memory_space=pltpu.VMEM), pl.BlockSpec(memory_space=pl.ANY)
    return pl.pallas_call(
        functools.partial(kernel, lats, lons),
        out_shape=pltpu.VMEM(features.shape, f32),
        in_specs=[anywhere] * 6,
        out_specs=vmem,
        scratch_shapes=[
            pltpu.SMEM(widths.shape, jnp.int32),
            pltpu.SMEM(tap_rows.shape, jnp.int32),
            pltpu.VMEM((1, channels), f32),
            pltpu.VMEM((TAPS, K, ROWS, SPAN), f32),
            pltpu.VMEM((3 * ROWS, channels // 2, L), f32),
            pltpu.VMEM((3 * ROWS, channels // 2, L), f32),
            pltpu.VMEM(weights.shape, f32),
            pltpu.VMEM((2, channels, K * channels // 2), bf16),
            pltpu.VMEM((2, channels, K * channels // 2), bf16),
            pltpu.VMEM((TAPS * K * ROWS, 2 * L), f32),
            pltpu.VMEM((TAPS * K * ROWS, 2 * L), f32),
            *(pltpu.VMEM((2 * TAPS * L, K * n * L), bf16) for n in (3, 2, 2, 2)),
            pltpu.VMEM((2, ROWS, channels // 2, 3 * TAPS * L), bf16),
            pltpu.VMEM((2, 2, K * channels // 2, WIDE), bf16),
            pltpu.VMEM((channels, CENTRES), f32),
            pltpu.VMEM((channels, L), f32),
            pltpu.VMEM((2, 2, channels, L), f32),
            pltpu.VMEM((2, 2, channels, L), f32),
            pltpu.SemaphoreType.DMA((2, 2 * ROWS)),
            pltpu.SemaphoreType.DMA((2, 3 * ROWS)),
            pltpu.SemaphoreType.DMA((2, 2)),
            pltpu.SemaphoreType.DMA((2, 2)),
            pltpu.SemaphoreType.DMA((2,)),
            pltpu.SemaphoreType.DMA,
            pltpu.SemaphoreType.DMA((4,)),
        ],
        compiler_params=pltpu.CompilerParams(
            collective_id=0, has_side_effects=True, vmem_limit_bytes=60 << 20
        ),
    )(widths, tap_rows, bias_term[None, :], jnp.transpose(basis_panels, (1, 2, 0, 3)), features, weights)


def solution(mesh):
    return jax.shard_map(
        functools.partial(per_device, mesh.shape["lat"], mesh.shape["lon"]),
        mesh=mesh,
        in_specs=(
            P("lat", None, "lon"),
            P("lat", None, None, None),
            P(),
            P(),
            P("lat"),
            P("lat", None),
        ),
        out_specs=P("lat", None, "lon"),
        check_vma=False,
    )
```
